32 devices in a mesh: grp: 8 (over y, x, core), pos: 4 (over z).
Axes of the slice: x: 2, y: 2, z: 4, core: 2. Of those that a mesh axis runs over, the one named last changes fastest.
Arguments:
- hidden_in: bfloat16 [16384, 768], P(('grp', 'pos')), may hold values from -6 to 6
- ln1_gain: bfloat16 [768], replicated, may hold values from 0.099609375 to 1.8984375
- ln1_shift: bfloat16 [768], replicated, may hold values from -1.75 to 1.75
- w_qkv: bfloat16 [768, 2304], replicated, may hold values from -0.21875 to 0.21875
- b_query: bfloat16 [768], replicated, may hold values from -3 to 3
- b_value: bfloat16 [768], replicated, may hold values from -1.75 to 1.75
- w_out: bfloat16 [768, 768], replicated, may hold values from -1.75 to 1.75
- b_out: bfloat16 [768], replicated, may hold values from -1.75 to 1.75
- ln2_gain: bfloat16 [768], replicated, may hold values from 0.099609375 to 1.8984375
- ln2_shift: bfloat16 [768], replicated, may hold values from -1.75 to 1.75
- w_up: bfloat16 [768, 3072], replicated, may hold values from -0.21875 to 0.21875
- b_up: bfloat16 [3072], replicated, may hold values from -1.75 to 1.75
- w_down: bfloat16 [3072, 768], replicated, may hold values from -0.109375 to 0.109375
- b_down: bfloat16 [768], replicated, may hold values from -1.75 to 1.75
- cotangent: bfloat16 [16384, 768], P(('grp', 'pos')), may hold values from -6 to 6
- sol_count: int32 [8], P('grp'), may hold values from 4 to 16, as said below
- prefix_len: int32 [8], P('grp'), may hold values from 128 to 512
- sol_len: int32 [8, 16], P('grp'), may hold values from 48 to 96, as said below
Outputs:
- layer_out: bfloat16 [16384, 768], P(('grp', 'pos'))
- input_grad: bfloat16 [16384, 768], P(('grp', 'pos'))
- grad_ln1_gain: float32 [768], replicated
- grad_ln1_shift: float32 [768], replicated
- grad_w_qkv: float32 [768, 2304], replicated
- grad_b_query: float32 [768], replicated
- grad_b_value: float32 [768], replicated
- grad_w_out: float32 [768, 768], replicated
- grad_b_out: float32 [768], replicated
- grad_ln2_gain: float32 [768], replicated
- grad_ln2_shift: float32 [768], replicated
- grad_w_up: float32 [768, 3072], replicated
- grad_b_up: float32 [3072], replicated
- grad_w_down: float32 [3072, 768], replicated
- grad_b_down: float32 [768], replicated
The draws below stay inside these ranges and needn't reach their ends.
Inputs may be any that keep to these rules, and one draw needn't show every extreme that they name: `sol_count`: each group has at least 4 solutions; the largest count is reached in every draw. `sol_len`: slots j with j >= sol_count of their group are unused; the lengths of a group never exceed 2048 in sum.
All inputs are finite; a program needn't handle non-finite values.
Results may differ from the reference program's by a relative error of at most 0.012.
Values may be sent and summed in bfloat16 or wider, within the bound.
No kernel may reach another device: no remote copies, remote signals or barrier semaphores. Data moves between devices by JAX's collectives and lax.ppermute only.
A program may use at most 256 MiB of HBM per device.

```python
import jax
import jax.numpy as jnp
from jax import lax

D = 768
HEADS = 12
HD = 64
FF = 3072
MAXSOL = 16
SET_LEN = 2048
SETS = 8
TOKENS = 16384


def chosen_sets(key):
    first = jax.random.randint(jax.random.fold_in(key, 71), (), 0, SETS)
    second = (first + 1) % SETS
    return (first, second)


def draw_sol_count(key, part):
    first, second = chosen_sets(key)
    counts = jax.random.randint(jax.random.fold_in(key, 11), (SETS,), 4, MAXSOL + 1)
    return counts.at[first].set(MAXSOL).at[second].set(4).astype(jnp.int32)


def draw_prefix_len(key, part):
    first, second = chosen_sets(key)
    lowest = SET_LEN // 16
    highest = SET_LEN // 4
    lengths = jax.random.randint(jax.random.fold_in(key, 12), (SETS,), lowest, highest + 1)
    return lengths.at[first].set(highest).at[second].set(lowest).astype(jnp.int32)


def draw_sol_len(key, part):
    first, second = chosen_sets(key)
    lowest = (SET_LEN - SET_LEN // 4) // 32
    highest = (SET_LEN - SET_LEN // 4) // 16
    lengths = jax.random.randint(jax.random.fold_in(key, 13), (SETS, MAXSOL), lowest, highest + 1)
    return lengths.at[first, 0].set(highest).at[second, 0].set(lowest).astype(jnp.int32)


def level_of(stream_key, dims, split, smallest, top_value):
    loudness = 1.0
    for axis_at, shards_of in split:
        draws = jax.random.uniform(jax.random.fold_in(jax.random.fold_in(stream_key, 6), axis_at), (shards_of,), jnp.float32, smallest / len(split), top_value / len(split))
        loudness = loudness * jnp.repeat(jnp.exp(draws), dims[axis_at] // shards_of).reshape((-1,) + (1,) * (len(dims) - 1 - axis_at))
    return loudness


def noise(key, dims, scale, bound, shards=(), held_as=jnp.bfloat16):
    drawn = scale * jax.random.normal(key, dims, jnp.float32)
    if shards:
        drawn = drawn * level_of(key, dims, shards, -0.22, 0.18)
    return jnp.clip(drawn, -bound, bound).astype(held_as)


def setup_inputs(seed: int = 0) -> dict:
    seeds = jax.random.split(jax.random.key(seed), 19)
    return {
        "hidden_in": noise(seeds[0], (TOKENS, D), 1.0, 6.0, ((0, 32),)),
        "ln1_gain": jnp.clip(1.0 + 0.18 * jax.random.normal(seeds[1], (D,), jnp.float32), 0.099609375, 1.8984375).astype(jnp.bfloat16),
        "ln1_shift": noise(seeds[2], (D,), 0.3, 1.75),
        "w_qkv": noise(seeds[3], (D, 3 * D), D ** -0.5, 0.21875),
        "b_query": noise(seeds[4], (D,), 0.5, 3.0),
        "b_value": noise(seeds[5], (D,), 0.3, 1.75),
        "w_out": noise(seeds[6], (D, D), (D // 64) ** -0.5, 1.75),
        "b_out": noise(seeds[7], (D,), 0.3, 1.75),
        "ln2_gain": jnp.clip(1.0 + 0.18 * jax.random.normal(seeds[8], (D,), jnp.float32), 0.099609375, 1.8984375).astype(jnp.bfloat16),
        "ln2_shift": noise(seeds[9], (D,), 0.3, 1.75),
        "w_up": noise(seeds[10], (D, FF), D ** -0.5, 0.21875),
        "b_up": noise(seeds[11], (FF,), 0.3, 1.75),
        "w_down": noise(seeds[12], (FF, D), FF ** -0.5, 0.109375),
        "b_down": noise(seeds[13], (D,), 0.3, 1.75),
        "cotangent": noise(seeds[14], (TOKENS, D), 1.0, 6.0, ((0, 32),)),
        "sol_count": draw_sol_count(jax.random.fold_in(seeds[18], 71), 0),
        "prefix_len": draw_prefix_len(jax.random.fold_in(seeds[18], 71), 0),
        "sol_len": draw_sol_len(jax.random.fold_in(seeds[18], 71), 0),
    }


@jax.custom_vjp
def low(v):
    return lax.optimization_barrier(v.astype(jnp.bfloat16)).astype(jnp.float32)

@jax.custom_vjp
def low_back(v):
    return v

def low_keep(v):
    return (low(v), None)

def low_pass(kept, grad):
    return (grad,)

def back_keep(v):
    return (v, None)

def back_low(kept, grad):
    return (low(grad),)
low.defvjp(low_keep, low_pass)
low_back.defvjp(back_keep, back_low)
eps_norm = 1e-05
neg_fill = -1e+30
highest = lax.Precision.HIGHEST

def round_both(values):
    return low(low_back(values))

def norm_rows(values, norm_gain, norm_shift):
    average = lax.optimization_barrier(jnp.mean(values, axis=-1, keepdims=True))
    centred = values - average
    spread = lax.optimization_barrier(jnp.mean(centred * centred, axis=-1, keepdims=True))
    return centred * lax.rsqrt(spread + eps_norm) * norm_gain + norm_shift

def segment_of(positions, sol_total, prefix, sol_lens):
    slot_ids = jnp.arange(sol_lens.shape[0], dtype=jnp.int32)
    lengths = jnp.concatenate([prefix.reshape(1), jnp.where(slot_ids < sol_total, sol_lens, 0)])
    seg_ends = jnp.cumsum(lengths)
    seg_starts = seg_ends - lengths
    segment = lax.optimization_barrier(jnp.sum((seg_starts[None, :] <= positions[:, None]).astype(jnp.int32), axis=1)) - 1
    return (segment, positions < seg_ends[-1])

def allowed_mask(query_pos, key_pos, sol_total, prefix, sol_lens):
    query_seg, query_real = segment_of(query_pos, sol_total, prefix, sol_lens)
    key_seg, key_real = segment_of(key_pos, sol_total, prefix, sol_lens)
    shared = (key_seg[None, :] == 0) | (key_seg[None, :] == query_seg[:, None])
    causal = key_pos[None, :] <= query_pos[:, None]
    inside = query_real[:, None] & key_real[None, :] & causal & shared
    return inside | (key_pos[None, :] == query_pos[:, None])

def attention(query, key, value, allowed):
    length = query.shape[0]

    def split_heads(matrix):
        return matrix.reshape(length, HEADS, HD).transpose(1, 0, 2)

    @jax.checkpoint
    def one_head(operands):
        head_q, head_k, head_v = operands
        scores = low_back(jnp.dot(head_q, head_k.T, precision=highest) * HD ** (-0.5))
        scores = jnp.where(allowed, scores, neg_fill)
        row_max = lax.optimization_barrier(jnp.max(scores, axis=-1, keepdims=True))
        expo = jnp.exp(scores - row_max)
        probs = low(expo / lax.optimization_barrier(jnp.sum(expo, axis=-1, keepdims=True)))
        return jnp.dot(probs, head_v, precision=highest)
    output = lax.map(one_head, (split_heads(query), split_heads(key), split_heads(value)))
    return output.transpose(1, 0, 2).reshape(length, HEADS * HD)

def layer(inputs, params, allowed):
    ln1_gain, ln1_shift, w_qkv, b_query, b_value, w_out, b_out, ln2_gain, ln2_shift, w_up, b_up, w_down, b_down = params
    normed1 = low(norm_rows(inputs, ln1_gain, ln1_shift))
    qkv = jnp.dot(normed1, w_qkv, precision=highest)
    query = round_both(qkv[:, :D] + b_query)
    key = round_both(qkv[:, D:2 * D])
    value = round_both(qkv[:, 2 * D:] + b_value)
    attended = round_both(attention(query, key, value, allowed))
    middle = inputs + low_back(jnp.dot(attended, w_out, precision=highest) + b_out)
    normed2 = low(norm_rows(middle, ln2_gain, ln2_shift))
    pre_act = low_back(jnp.dot(normed2, w_up, precision=highest) + b_up)
    activ = low(jax.nn.gelu(pre_act, approximate=True))
    return middle + low_back(jnp.dot(activ, w_down, precision=highest) + b_down)

def reference(hidden_in, ln1_gain, ln1_shift, w_qkv, b_query, b_value, w_out, b_out, ln2_gain, ln2_shift, w_up, b_up, w_down, b_down, cotangent, sol_count, prefix_len, sol_len):
    params = tuple((p.astype(jnp.float32) for p in (ln1_gain, ln1_shift, w_qkv, b_query, b_value, w_out, b_out, ln2_gain, ln2_shift, w_up, b_up, w_down, b_down)))
    inputs_all = hidden_in.astype(jnp.float32).reshape(SETS, SET_LEN, D)
    grads_all = cotangent.astype(jnp.float32).reshape(SETS, SET_LEN, D)
    positions = jnp.arange(SET_LEN, dtype=jnp.int32)

    def one_set(totals, item):
        inputs, upstream, sol_total, prefix, sol_lens = item
        allowed = allowed_mask(positions, positions, sol_total, prefix, sol_lens)
        output, pullback = jax.vjp(lambda xin, pin: layer(xin, pin, allowed), inputs, params)
        input_grad, param_grads = pullback(upstream)
        totals = tuple((a + b for a, b in zip(totals, param_grads)))
        return (totals, (output.astype(jnp.bfloat16), input_grad.astype(jnp.bfloat16)))
    zeros = tuple((jnp.zeros_like(p) for p in params))
    totals, (outputs, input_grads) = lax.scan(one_set, zeros, (inputs_all, grads_all, sol_count, prefix_len, sol_len))
    return (outputs.reshape(TOKENS, D), input_grads.reshape(TOKENS, D), totals[0], totals[1], totals[2], totals[3], totals[4], totals[5], totals[6], totals[7], totals[8], totals[9], totals[10], totals[11], totals[12])
```

```python
import functools

import jax
import jax.numpy as jnp
from jax import lax
from jax.experimental import pallas as pl
from jax.experimental.pallas import tpu as pltpu
from jax.sharding import PartitionSpec as P

HD = 64
BQ = 128
SLABS = 8
PIECES = 4
ROWS = 96
EXTRA = 8

eps_norm = 1e-05
neg_fill = -1e30
f32 = jnp.float32
bf16 = jnp.bfloat16


def dot(a, b, dims):
    return lax.dot_general(a, b, (dims, ((), ())), preferred_element_type=f32)


NN = ((1,), (0,))
NT = ((1,), (1,))
TN = ((0,), (0,))


def norm_stats(values):
    average = jnp.mean(values, axis=-1, keepdims=True)
    centred = values - average
    spread = jnp.mean(centred * centred, axis=-1, keepdims=True)
    inv = lax.rsqrt(spread + eps_norm)
    return centred * inv, inv


def norm_back(grad, gain, xhat, inv):
    e = grad * gain
    return inv * (
        e
        - jnp.mean(e, axis=-1, keepdims=True)
        - xhat * jnp.mean(e * xhat, axis=-1, keepdims=True)
    )


def gelu_tanh(values):
    return jax.nn.gelu(values, approximate=True)


def column_sum(gradient):
    return jnp.sum(gradient.astype(f32), axis=0)


def fill_bias(pos_ref, count_ref, prefix_ref, lens_ref, bias_a, bias_b, rows, reach, tail):
    first = pos_ref[0] * rows
    blocks = rows // BQ
    qpos = first + lax.broadcasted_iota(jnp.int32, (8, rows), 1)
    prefix = prefix_ref[0]
    start = prefix
    seg_start = jnp.where(qpos >= start, start, 0)
    for j in range(lens_ref.shape[1]):
        start = start + jnp.where(j < count_ref[0], lens_ref[0, j], 0)
        seg_start = jnp.where(qpos >= start, start, seg_start)
    real = qpos < start
    seg_start = jnp.where(real, seg_start, qpos)[:1]
    low = jnp.where(real, prefix, 0)[:1]
    qpos = qpos[:1]
    for b in range(blocks):
        at = slice(BQ * b, BQ * b + BQ)
        kpos = lax.broadcasted_iota(jnp.int32, (reach, BQ), 0)
        ok = (kpos <= qpos[:, at]) & ((kpos < low[:, at]) | (kpos >= seg_start[:, at]))
        bias_a[b] = jnp.where(ok, 0.0, neg_fill)
        kpos = first + BQ * b - tail + lax.broadcasted_iota(jnp.int32, (tail + BQ, BQ), 0)
        ok = (kpos <= qpos[:, at]) & (kpos >= seg_start[:, at]) & (kpos >= reach)
        bias_b[b] = jnp.where(ok, 0.0, neg_fill)


def transposed(x):
    return x.astype(f32).T.astype(bf16)


def head_part(x, h):
    lane = lax.broadcasted_iota(jnp.int32, x.shape, 1)
    return jnp.where((lane >= h * HD) & (lane < (h + 1) * HD), x, jnp.zeros_like(x))


def attend_kernel(
    pos_ref, count_ref, prefix_ref, lens_ref,
    q_ref, k_ref, v_ref, kx_ref, vx_ref,
    out_ref, lse_ref,
    bias_a, bias_b, k_ext, v_ext_t, v0_t,
    *, rows, reach, tail,
):
    @pl.when(pl.program_id(0) == 0)
    def _():
        fill_bias(pos_ref, count_ref, prefix_ref, lens_ref, bias_a, bias_b, rows, reach, tail)

    blocks = rows // BQ
    k_ext[:tail] = kx_ref[:tail]
    k_ext[tail:] = k_ref[...]
    v_ext_t[:, :tail] = transposed(vx_ref[:tail])
    v_ext_t[:, tail:] = transposed(v_ref[...])
    v0_t[...] = transposed(vx_ref[tail:])
    k0 = kx_ref[tail:]
    for b in range(blocks):
        query = q_ref[BQ * b : BQ * b + BQ, :] * jnp.asarray(HD**-0.5, bf16)
        k_band = k_ext[BQ * b : BQ * b + BQ + tail, :]
        outs = []
        for h in range(2):
            part = head_part(query, h)
            s_a = dot(k0, part, NT) + bias_a[b]
            s_b = dot(k_band, part, NT) + bias_b[b]
            top = jnp.maximum(
                jnp.max(s_a, axis=0, keepdims=True), jnp.max(s_b, axis=0, keepdims=True)
            )
            p_a = jnp.exp(s_a - top)
            p_b = jnp.exp(s_b - top)
            total = jnp.sum(p_a, axis=0, keepdims=True) + jnp.sum(p_b, axis=0, keepdims=True)
            hs = slice(h * HD, h * HD + HD)
            o = dot(v0_t[hs, :], p_a.astype(bf16), NN) + dot(
                v_ext_t[hs, BQ * b : BQ * b + BQ + tail], p_b.astype(bf16), NN
            )
            outs.append(o * (1.0 / total))
            lse_ref[0, b, h : h + 1, :] = top + jnp.log(total)
        out_ref[BQ * b : BQ * b + BQ, :] = jnp.concatenate(outs, axis=0).T.astype(bf16)


def attend_back_kernel(
    pos_ref, count_ref, prefix_ref, lens_ref,
    q_ref, k_ref, v_ref, kx_ref, vx_ref, g_ref, lse_ref,
    dq_ref, dk_ref, dv_ref, dkx_ref, dvx_ref,
    bias_a, bias_b, k_ext, v_ext, k_ext_t, k0_t, dk_ext, dv_ext, dk0, dv0,
    *, rows, reach, tail,
):
    @pl.when(pl.program_id(0) == 0)
    def _():
        fill_bias(pos_ref, count_ref, prefix_ref, lens_ref, bias_a, bias_b, rows, reach, tail)

    blocks = rows // BQ
    k_ext[:tail] = kx_ref[:tail]
    k_ext[tail:] = k_ref[...]
    v_ext[:tail] = vx_ref[:tail]
    v_ext[tail:] = v_ref[...]
    k_ext_t[:, :tail] = transposed(kx_ref[:tail])
    k_ext_t[:, tail:] = transposed(k_ref[...])
    k0_t[...] = transposed(kx_ref[tail:])
    k0 = kx_ref[tail:]
    v0 = vx_ref[tail:]
    dk_ext[...] = jnp.zeros_like(dk_ext)
    dv_ext[...] = jnp.zeros_like(dv_ext)
    scale = HD**-0.5
    for b in range(blocks):
        at = slice(BQ * b, BQ * b + BQ)
        band = slice(BQ * b, BQ * b + BQ + tail)
        query = q_ref[at, :] * jnp.asarray(scale, bf16)
        grad = g_ref[at, :]
        k_band = k_ext[band, :]
        v_band = v_ext[band, :]
        outs = []
        for h in range(2):
            hs = slice(h * HD, h * HD + HD)
            part = head_part(query, h)
            gpart = head_part(grad, h)
            lse = lse_ref[0, b, h : h + 1, :]
            p_a = jnp.exp(dot(k0, part, NT) + bias_a[b] - lse)
            p_b = jnp.exp(dot(k_band, part, NT) + bias_b[b] - lse)
            dp_a = dot(v0, gpart, NT)
            dp_b = dot(v_band, gpart, NT)
            inner = jnp.sum(p_a * dp_a, axis=0, keepdims=True) + jnp.sum(
                p_b * dp_b, axis=0, keepdims=True
            )
            ds_a = (p_a * (dp_a - inner)).astype(bf16)
            ds_b = (p_b * (dp_b - inner)).astype(bf16)
            dv_a = dot(p_a.astype(bf16), gpart, NN)
            dk_a = dot(ds_a, part, NN)
            if b == 0 and h == 0:
                dv0[...] = dv_a
                dk0[...] = dk_a
            else:
                dv0[...] += dv_a
                dk0[...] += dk_a
            dv_ext[band, :] += dot(p_b.astype(bf16), gpart, NN)
            dk_ext[band, :] += dot(ds_b, part, NN)
            outs.append(dot(k0_t[hs, :], ds_a, NN) + dot(k_ext_t[hs, band], ds_b, NN))
        dq_ref[at, :] = (jnp.concatenate(outs, axis=0) * scale).T.astype(bf16)
    dkx_ref[:tail] = dk_ext[:tail].astype(bf16)
    dkx_ref[tail:] = dk0[...].astype(bf16)
    dvx_ref[:tail] = dv_ext[:tail].astype(bf16)
    dvx_ref[tail:] = dv0[...].astype(bf16)
    dk_ref[...] = dk_ext[tail:].astype(bf16)
    dv_ref[...] = dv_ext[tail:].astype(bf16)


def column_block(rows, offset=0):
    return pl.BlockSpec((rows, 128), lambda i, *_: (0, offset + i))


def attend(scalars, qkv, kvx, rows, reach, tail):
    width = qkv.shape[1] // 3
    steps = width // 128
    blocks = rows // BQ
    extra = reach + tail
    return pl.pallas_call(
        functools.partial(attend_kernel, rows=rows, reach=reach, tail=tail),
        grid_spec=pltpu.PrefetchScalarGridSpec(
            num_scalar_prefetch=4,
            grid=(steps,),
            in_specs=[
                column_block(rows),
                column_block(rows, steps),
                column_block(rows, 2 * steps),
                column_block(extra),
                column_block(extra, steps),
            ],
            out_specs=[
                column_block(rows),
                pl.BlockSpec((1, blocks, 2, BQ), lambda i, *_: (i, 0, 0, 0)),
            ],
            scratch_shapes=[
                pltpu.VMEM((blocks, reach, BQ), f32),
                pltpu.VMEM((blocks, tail + BQ, BQ), f32),
                pltpu.VMEM((tail + rows, 128), bf16),
                pltpu.VMEM((128, tail + rows), bf16),
                pltpu.VMEM((128, reach), bf16),
            ],
        ),
        out_shape=[
            jax.ShapeDtypeStruct((rows, width), bf16),
            jax.ShapeDtypeStruct((steps, blocks, 2, BQ), f32),
        ],
        name="attend",
    )(*scalars, qkv, qkv, qkv, kvx, kvx)


def attend_back(scalars, qkv, kvx, grad, lse, rows, reach, tail):
    width = qkv.shape[1] // 3
    steps = width // 128
    blocks = rows // BQ
    extra = reach + tail
    return pl.pallas_call(
        functools.partial(attend_back_kernel, rows=rows, reach=reach, tail=tail),
        grid_spec=pltpu.PrefetchScalarGridSpec(
            num_scalar_prefetch=4,
            grid=(steps,),
            in_specs=[
                column_block(rows),
                column_block(rows, steps),
                column_block(rows, 2 * steps),
                column_block(extra),
                column_block(extra, steps),
                column_block(rows),
                pl.BlockSpec((1, blocks, 2, BQ), lambda i, *_: (i, 0, 0, 0)),
            ],
            out_specs=[
                column_block(rows),
                column_block(rows),
                column_block(rows),
                column_block(extra),
                column_block(extra),
            ],
            scratch_shapes=[
                pltpu.VMEM((blocks, reach, BQ), f32),
                pltpu.VMEM((blocks, tail + BQ, BQ), f32),
                pltpu.VMEM((tail + rows, 128), bf16),
                pltpu.VMEM((tail + rows, 128), bf16),
                pltpu.VMEM((128, tail + rows), bf16),
                pltpu.VMEM((128, reach), bf16),
                pltpu.VMEM((tail + rows, 128), f32),
                pltpu.VMEM((tail + rows, 128), f32),
                pltpu.VMEM((reach, 128), f32),
                pltpu.VMEM((reach, 128), f32),
            ],
        ),
        out_shape=[
            jax.ShapeDtypeStruct((rows, width), bf16),
            jax.ShapeDtypeStruct((rows, width), bf16),
            jax.ShapeDtypeStruct((rows, width), bf16),
            jax.ShapeDtypeStruct((extra, width), bf16),
            jax.ShapeDtypeStruct((extra, width), bf16),
        ],
        name="attend_back",
    )(*scalars, qkv, qkv, qkv, kvx, kvx, grad, lse)


def mask_of(side, me):
    return me[1] + side * (me[2] - me[1])


def slab_at(place, me):
    side = (place >> 2) ^ me[0]
    return (side << 2) | ((place & 3) ^ mask_of(side, me))


def place_of(slab, me):
    side = slab >> 2
    return ((side ^ me[0]) << 2) | ((slab & 3) ^ mask_of(side, me))


def slab_rows(result, me_ref, out_ref):
    for c in range(PIECES):
        out_ref[0, c ^ (me_ref[3]), :ROWS, :] = result[ROWS * c : ROWS * c + ROWS].astype(bf16)


def outer_kernel(me_ref, a_ref, b_ref, out_ref):
    slab_rows(dot(a_ref[...], b_ref[...], TN), me_ref, out_ref)


def outer_half(me, a, b, half):
    rows, many = a.shape
    wide = many // SLABS
    return pl.pallas_call(
        outer_kernel,
        grid_spec=pltpu.PrefetchScalarGridSpec(
            num_scalar_prefetch=1,
            grid=(4,),
            in_specs=[
                pl.BlockSpec((rows, wide), lambda r, me: (0, slab_at(r + 4 * half, me))),
                pl.BlockSpec(b.shape, lambda r, me: (0, 0)),
            ],
            out_specs=pl.BlockSpec((1, PIECES, ROWS, b.shape[1]), lambda r, me: (r, 0, 0, 0)),
        ),
        out_shape=jax.ShapeDtypeStruct((4, PIECES, ROWS, b.shape[1]), bf16),
        name="outer",
    )(me, a, b)


def mixed_kernel(
    me_ref, dqkv_ref, n_ref, dkvx_ref, nx_ref, att_ref, gb_ref, small_ref, out_ref, *, half
):
    o = slab_at(pl.program_id(0) + 4 * half, me_ref)

    @pl.when(o < 2)
    def _():
        slab_rows(dot(dqkv_ref[...], n_ref[...], TN), me_ref, out_ref)

    @pl.when((o >= 2) & (o < 6))
    def _():
        slab_rows(
            dot(dqkv_ref[...], n_ref[...], TN) + dot(dkvx_ref[...], nx_ref[...], TN),
            me_ref,
            out_ref,
        )

    @pl.when(o >= 6)
    def _():
        slab_rows(dot(att_ref[...], gb_ref[...], TN), me_ref, out_ref)

    for c in range(PIECES):
        value = small_ref[EXTRA * c : EXTRA * c + EXTRA] if c < 2 else jnp.zeros_like(small_ref[:EXTRA])
        out_ref[0, c ^ (me_ref[3]), ROWS:, :] = jnp.where(o == 0, value, 0.0).astype(bf16)


def mixed_half(me, dqkv, normed, dkvx, normed_x, attended, grad_branch, small, half):
    rows, width = normed.shape
    wide = width // 2

    def slab(r, me):
        return slab_at(r + 4 * half, me)

    whole = lambda x: pl.BlockSpec(x.shape, lambda r, me: (0, 0))
    return pl.pallas_call(
        functools.partial(mixed_kernel, half=half),
        grid_spec=pltpu.PrefetchScalarGridSpec(
            num_scalar_prefetch=1,
            grid=(4,),
            in_specs=[
                pl.BlockSpec((rows, wide), lambda r, me: (0, jnp.minimum(slab(r, me), 5))),
                whole(normed),
                pl.BlockSpec(
                    (dkvx.shape[0], wide), lambda r, me: (0, jnp.clip(slab(r, me) - 2, 0, 3))
                ),
                whole(normed_x),
                pl.BlockSpec((rows, wide), lambda r, me: (0, jnp.maximum(slab(r, me) - 6, 0))),
                whole(grad_branch),
                whole(small),
            ],
            out_specs=pl.BlockSpec(
                (1, PIECES, ROWS + EXTRA, width), lambda r, me: (r, 0, 0, 0)
            ),
        ),
        out_shape=jax.ShapeDtypeStruct((4, PIECES, ROWS + EXTRA, width), bf16),
        name="outer_mixed",
    )(me, dqkv, normed, dkvx, normed_x, attended, grad_branch, small)


def slab_of(me_ref, f_ref, g_ref, o):
    far = (o >> 2) != me_ref[0]
    low = me_ref[3]
    pieces = []
    for c in range(PIECES):
        f = f_ref[0, c ^ low, :ROWS, :].astype(f32)
        g = g_ref[0, c ^ low, :ROWS, :].astype(f32)
        pieces.append(jnp.where(far, g, f))
    return jnp.concatenate(pieces, axis=0)


def spread_kernel(me_ref, f_ref, g_ref, out_ref, *, turned):
    slab = slab_of(me_ref, f_ref, g_ref, pl.program_id(0))
    out_ref[...] = slab.T if turned else slab


def half_specs(rows, width):
    spec = pl.BlockSpec((1, PIECES, rows, width), lambda o, me: (place_of(o, me) & 3, 0, 0, 0))
    return [spec, spec]


def spread(me, near, far, turned):
    width = near.shape[-1]
    wide = PIECES * ROWS
    many = SLABS * wide
    return pl.pallas_call(
        functools.partial(spread_kernel, turned=turned),
        grid_spec=pltpu.PrefetchScalarGridSpec(
            num_scalar_prefetch=1,
            grid=(SLABS,),
            in_specs=half_specs(ROWS, width),
            out_specs=pl.BlockSpec((width, wide), lambda o, me: (0, o))
            if turned
            else pl.BlockSpec((wide, width), lambda o, me: (o, 0)),
        ),
        out_shape=jax.ShapeDtypeStruct((width, many) if turned else (many, width), f32),
        name="spread",
    )(me, near, far)


def mixed_spread_kernel(me_ref, f_ref, g_ref, qkv_ref, out_ref, small_ref):
    o = pl.program_id(0)
    slab = slab_of(me_ref, f_ref, g_ref, o)

    @pl.when(o < 6)
    def _():
        qkv_ref[...] = slab.T

    @pl.when(o >= 6)
    def _():
        out_ref[...] = slab

    @pl.when(o == 0)
    def _():
        far = me_ref[0] != 0
        for c in range(2):
            at = c ^ (me_ref[3])
            f = f_ref[0, at, ROWS:, :].astype(f32)
            g = g_ref[0, at, ROWS:, :].astype(f32)
            small_ref[EXTRA * c : EXTRA * c + EXTRA, :] = jnp.where(far, g, f)


def mixed_spread(me, near, far):
    width = near.shape[-1]
    wide = PIECES * ROWS
    return pl.pallas_call(
        mixed_spread_kernel,
        grid_spec=pltpu.PrefetchScalarGridSpec(
            num_scalar_prefetch=1,
            grid=(SLABS,),
            in_specs=half_specs(ROWS + EXTRA, width),
            out_specs=[
                pl.BlockSpec((width, wide), lambda o, me: (0, jnp.minimum(o, 5))),
                pl.BlockSpec((wide, width), lambda o, me: (jnp.maximum(o - 6, 0), 0)),
                pl.BlockSpec((2 * EXTRA, width), lambda o, me: (0, 0)),
            ],
        ),
        out_shape=[
            jax.ShapeDtypeStruct((width, 3 * width), f32),
            jax.ShapeDtypeStruct((width, width), f32),
            jax.ShapeDtypeStruct((2 * EXTRA, width), f32),
        ],
        name="mixed_spread",
    )(me, near, far)


def grp_pairs(step):
    return [(g, step(g)) for g in range(8)]


ROUTES = (
    ("grp", grp_pairs(lambda g: g ^ 1)),
    ("grp", grp_pairs(lambda g: g ^ (2 if g % 2 == 0 else 4))),
    ("grp", grp_pairs(lambda g: g ^ (4 if g % 2 == 0 else 2))),
    ("pos", [(p, p ^ 1) for p in range(4)]),
    ("pos", [(p, p ^ 2) for p in range(4)]),
)


def hop(value, step):
    axis, pairs = ROUTES[step]
    return lax.ppermute(value, axis, pairs)


def added(a, b):
    return (a.astype(f32) + b.astype(f32)).astype(bf16)


def total_halves(near, far, cube):
    if not cube:
        return lax.psum((near, far), ("grp", "pos"))
    shape = near.shape
    count = shape[0] * shape[1]
    keep = near.reshape((count,) + shape[2:])
    send = far.reshape((count,) + shape[2:])
    for step in range(5):
        got = hop(send, step)
        half = count // 2
        if step < 4:
            send = added(keep[half:], got[half:])
            keep = added(keep[:half], got[:half])
            count = half
        else:
            keep = added(keep, got)
    for step in (4, 3, 2, 1):
        keep = jnp.concatenate([keep, hop(keep, step)], axis=0)
    other = hop(keep, 0)
    return keep.reshape(shape), other.reshape(shape)


def fetch_first(value, blocks, cube):
    if cube and blocks == 1:
        place = lax.axis_index("pos")
        got = lax.ppermute(value, "pos", [(0, 2)])
        here = jnp.where(place == 2, got, value)
        got = lax.ppermute(here, "pos", [(0, 1), (2, 3)])
        return jnp.where(place % 2 == 1, got, here)
    rows = value.shape[0]
    return lax.all_gather(value, "pos", axis=0, tiled=True)[: blocks * rows]


def return_first(partial, blocks, rows, cube):
    place = lax.axis_index("pos")
    if cube and blocks == 1:
        low = partial.astype(bf16)
        here = partial.astype(f32) + lax.ppermute(low, "pos", [(1, 0), (3, 2)]).astype(f32)
        got = lax.ppermute(here.astype(bf16), "pos", [(2, 0)])
        mine = here + got.astype(f32)
    else:
        total = lax.psum(partial.astype(bf16), "pos")
        at = jnp.minimum(place, blocks - 1) * rows
        mine = lax.dynamic_slice_in_dim(total, at, rows, axis=0).astype(f32)
    return jnp.where(place < blocks, mine, 0.0)


def body(
    hidden_in,
    ln1_gain,
    ln1_shift,
    w_qkv,
    b_query,
    b_value,
    w_out,
    b_out,
    ln2_gain,
    ln2_shift,
    w_up,
    b_up,
    w_down,
    b_down,
    cotangent,
    sol_count,
    prefix_len,
    sol_len,
):
    rows, width = hidden_in.shape
    n_pos = lax.axis_size("pos")
    n_grp = lax.axis_size("grp")
    cube = n_grp == 8 and n_pos == 4
    set_length = rows * n_pos
    blocks = -(-(set_length // 4) // rows)
    reach = blocks * rows
    tail = -(-(3 * set_length // 64) // BQ) * BQ

    place = lax.axis_index("pos")
    if cube:
        g = lax.axis_index("grp")
        core, x, y = g & 1, (g >> 1) & 1, (g >> 2) & 1
        me = jnp.stack([core, 2 * x + y, 2 * y + x, 2 * (place & 1) + (place >> 1)])
    else:
        me = jnp.zeros((4,), jnp.int32)
    me = me.astype(jnp.int32)
    scalars = (place.astype(jnp.int32).reshape(1), sol_count, prefix_len, sol_len)

    gain1, shift1 = ln1_gain.astype(f32), ln1_shift.astype(f32)
    gain2, shift2 = ln2_gain.astype(f32), ln2_shift.astype(f32)

    tail_in = lax.ppermute(
        hidden_in[rows - tail :], "pos", [(p, p + 1) for p in range(n_pos - 1)]
    )
    first_in = fetch_first(hidden_in, blocks, cube)

    inputs = hidden_in.astype(f32)
    xhat1, inv1 = norm_stats(inputs)
    normed1 = (xhat1 * gain1 + shift1).astype(bf16)
    bias = jnp.concatenate([b_query.astype(f32), jnp.zeros((width,), f32), b_value.astype(f32)])
    qkv = (dot(normed1, w_qkv, NN) + bias).astype(bf16)

    inputs_x = jnp.concatenate([tail_in, first_in], axis=0).astype(f32)
    xhat1_x, _ = norm_stats(inputs_x)
    normed1_x = (xhat1_x * gain1 + shift1).astype(bf16)
    kvx = (dot(normed1_x, w_qkv[:, width:], NN) + bias[width:]).astype(bf16)

    attended, lse = attend(scalars, qkv, kvx, rows, reach, tail)

    middle = inputs + dot(attended, w_out, NN) + b_out.astype(f32)
    xhat2, inv2 = norm_stats(middle)
    normed2 = (xhat2 * gain2 + shift2).astype(bf16)
    pre_act = dot(normed2, w_up, NN) + b_up.astype(f32)
    activ, gelu_pull = jax.vjp(gelu_tanh, pre_act)
    activ = activ.astype(bf16)

    down_far = outer_half(me, activ, cotangent, 1)
    down_near = outer_half(me, activ, cotangent, 0)
    down = total_halves(down_near, down_far, cube)

    grad_activ = dot(cotangent, w_down, NT)
    grad_pre = gelu_pull(grad_activ)[0].astype(bf16)

    up_far = outer_half(me, grad_pre, normed2, 1)
    up_near = outer_half(me, grad_pre, normed2, 0)
    up = total_halves(up_near, up_far, cube)

    grad_normed2 = dot(grad_pre, w_up, NT)
    grad_middle = cotangent.astype(f32) + norm_back(grad_normed2, gain2, xhat2, inv2)
    grad_branch = grad_middle.astype(bf16)
    grad_attended = dot(grad_branch, w_out, NT).astype(bf16)
    dq, dk, dv, dkx, dvx = attend_back(
        scalars, qkv, kvx, grad_attended, lse, rows, reach, tail
    )
    dqkv = jnp.concatenate([dq, dk, dv], axis=1)
    dkvx = jnp.concatenate([dkx, dvx], axis=1)
    grad_normed1 = dot(dqkv, w_qkv, NT)
    grad_normed1_x = dot(dkvx, w_qkv[:, width:], NT)

    small = jnp.concatenate(
        [
            column_sum(cotangent),
            column_sum(grad_pre),
            column_sum(grad_normed2 * xhat2),
            column_sum(grad_normed2),
            column_sum(grad_branch),
            column_sum(dq),
            column_sum(dv) + column_sum(dvx),
            column_sum(grad_normed1 * xhat1) + column_sum(grad_normed1_x * xhat1_x),
            column_sum(grad_normed1) + column_sum(grad_normed1_x),
            jnp.zeros((4 * width,), f32),
        ]
    ).reshape(2 * EXTRA, width)
    mixed_args = (me, dqkv, normed1, dkvx, normed1_x, attended, grad_branch, small)
    mixed_far = mixed_half(*mixed_args, 1)
    mixed_near = mixed_half(*mixed_args, 0)
    mixed = total_halves(mixed_near, mixed_far, cube)

    back_tail = lax.ppermute(
        grad_normed1_x[:tail].astype(bf16), "pos", [(p + 1, p) for p in range(n_pos - 1)]
    )
    back_first = return_first(grad_normed1_x[tail:], blocks, rows, cube)
    grad_normed1 = (
        grad_normed1
        + back_first
        + jnp.concatenate([jnp.zeros((rows - tail, width), f32), back_tail.astype(f32)], axis=0)
    )
    input_grad = (grad_middle + norm_back(grad_normed1, gain1, xhat1, inv1)).astype(bf16)

    layer_out = (middle + dot(activ, w_down, NN) + b_down.astype(f32)).astype(bf16)

    grad_w_down = spread(me, *down, False)
    grad_w_up = spread(me, *up, True)
    grad_w_qkv, grad_w_out, vectors = mixed_spread(me, *mixed)
    return (
        layer_out,
        input_grad,
        vectors[10],
        vectors[11],
        grad_w_qkv,
        vectors[8],
        vectors[9],
        grad_w_out,
        vectors[7],
        vectors[5],
        vectors[6],
        grad_w_up,
        vectors[1:5].reshape(-1),
        grad_w_down,
        vectors[0],
    )


def solution(mesh):
    rows = P(("grp", "pos"), None)
    placed = (rows,) + (P(),) * 13 + (rows, P("grp"), P("grp"), P("grp", None))
    return jax.shard_map(
        body,
        mesh=mesh,
        in_specs=placed,
        out_specs=(rows, rows) + (P(),) * 13,
        check_vma=False,
    )
```

```python
import functools

import jax
import jax.numpy as jnp
from jax import lax
from jax.experimental import pallas as pl
from jax.experimental.pallas import tpu as pltpu
from jax.sharding import PartitionSpec as P

HD = 64
BQ = 128
SLABS = 8
PIECES = 4
ROWS = 96
EXTRA = 8

eps_norm = 1e-05
neg_fill = -1e30
f32 = jnp.float32
bf16 = jnp.bfloat16


def dot(a, b, dims):
    return lax.dot_general(a, b, (dims, ((), ())), preferred_element_type=f32)


NN = ((1,), (0,))
NT = ((1,), (1,))
TN = ((0,), (0,))


def norm_stats(values):
    average = jnp.mean(values, axis=-1, keepdims=True)
    centred = values - average
    spread = jnp.mean(centred * centred, axis=-1, keepdims=True)
    inv = lax.rsqrt(spread + eps_norm)
    return centred * inv, inv


def norm_back(grad, gain, xhat, inv):
    e = grad * gain
    return inv * (
        e
        - jnp.mean(e, axis=-1, keepdims=True)
        - xhat * jnp.mean(e * xhat, axis=-1, keepdims=True)
    )


def gelu_tanh(values):
    return jax.nn.gelu(values, approximate=True)


def column_sum(gradient):
    return jnp.sum(gradient.astype(f32), axis=0)


def fill_bias(pos_ref, count_ref, prefix_ref, lens_ref, bias_a, bias_b, rows, reach, tail):
    first = pos_ref[0] * rows
    blocks = rows // BQ
    qpos = first + lax.broadcasted_iota(jnp.int32, (8, rows), 1)
    prefix = prefix_ref[0]
    start = prefix
    seg_start = jnp.where(qpos >= start, start, 0)
    for j in range(lens_ref.shape[1]):
        start = start + jnp.where(j < count_ref[0], lens_ref[0, j], 0)
        seg_start = jnp.where(qpos >= start, start, seg_start)
    real = qpos < start
    seg_start = jnp.where(real, seg_start, qpos)[:1]
    low = jnp.where(real, prefix, 0)[:1]
    qpos = qpos[:1]
    for b in range(blocks):
        at = slice(BQ * b, BQ * b + BQ)
        kpos = lax.broadcasted_iota(jnp.int32, (reach, BQ), 0)
        ok = (kpos <= qpos[:, at]) & ((kpos < low[:, at]) | (kpos >= seg_start[:, at]))
        bias_a[b] = jnp.where(ok, 0.0, neg_fill)
        kpos = first + BQ * b - tail + lax.broadcasted_iota(jnp.int32, (tail + BQ, BQ), 0)
        ok = (kpos <= qpos[:, at]) & (kpos >= seg_start[:, at]) & (kpos >= reach)
        bias_b[b] = jnp.where(ok, 0.0, neg_fill)


def transposed(x):
    return x.astype(f32).T.astype(bf16)


def head_part(x, h):
    lane = lax.broadcasted_iota(jnp.int32, x.shape, 1)
    return jnp.where((lane >= h * HD) & (lane < (h + 1) * HD), x, jnp.zeros_like(x))


def both_heads(x):
    return jnp.concatenate([head_part(x, 0), head_part(x, 1)], axis=0)


def twice(x):
    return jnp.concatenate([x, x], axis=1)


def key_chunks(reach, tail, b):
    first = [(True, slice(c, c + 128), slice(c, c + 128)) for c in range(0, reach, 128)]
    band = [
        (False, slice(BQ * b + c, BQ * b + c + 128), slice(c, c + 128))
        for c in range(0, tail + BQ, 128)
    ]
    return first + band


def attend_kernel(
    pos_ref, count_ref, prefix_ref, lens_ref,
    q_ref, k_ref, v_ref, kx_ref, vx_ref,
    out_ref, turned_ref, lse_ref,
    bias_a, bias_b, k_ext, v_ext_t, v0_t, scores,
    *, rows, reach, tail,
):
    @pl.when(pl.program_id(0) == 0)
    def _():
        fill_bias(pos_ref, count_ref, prefix_ref, lens_ref, bias_a, bias_b, rows, reach, tail)

    k_ext[:tail] = kx_ref[:tail]
    k_ext[tail:] = k_ref[...]
    v_ext_t[:, :tail] = transposed(vx_ref[:tail])
    v_ext_t[:, tail:] = transposed(v_ref[...])
    v0_t[...] = transposed(vx_ref[tail:])
    for b in range(rows // BQ):
        at = slice(BQ * b, BQ * b + BQ)
        parts = both_heads(q_ref[at, :] * jnp.asarray(HD**-0.5, bf16))
        chunks = key_chunks(reach, tail, b)
        tops = None
        for i, (first, keys, biased) in enumerate(chunks):
            k = kx_ref[tail + keys.start : tail + keys.stop] if first else k_ext[keys, :]
            bias = bias_a[b, biased] if first else bias_b[b, biased]
            s = dot(k, parts, NT) + twice(bias)
            scores[b % 2, 128 * i : 128 * i + 128, :] = s
            s = jnp.max(s.reshape(16, 8, 2 * BQ), axis=0)
            tops = s if tops is None else jnp.maximum(tops, s)
        top = jnp.max(tops, axis=0, keepdims=True)
        sums = None
        o = None
        for i, (first, keys, _) in enumerate(chunks):
            p = jnp.exp(scores[b % 2, 128 * i : 128 * i + 128, :] - top)
            q = jnp.sum(p.reshape(16, 8, 2 * BQ), axis=0)
            sums = q if sums is None else sums + q
            v = v0_t[:, keys] if first else v_ext_t[:, keys]
            p = dot(v, p.astype(bf16), NN)
            o = p if o is None else o + p
        total = jnp.sum(sums, axis=0, keepdims=True)
        o = o * (1.0 / total)
        o = jnp.concatenate([o[:HD, :BQ], o[HD:, BQ:]], axis=0)
        turned_ref[0, b] = o
        lse_ref[0, b] = top + jnp.log(total)
        out_ref[at, :] = o.T.astype(bf16)


def attend_back_kernel(
    pos_ref, count_ref, prefix_ref, lens_ref,
    q_ref, k_ref, v_ref, kx_ref, vx_ref, g_ref, turned_ref, lse_ref,
    dq_ref, dk_ref, dv_ref, dkx_ref, dvx_ref,
    bias_a, bias_b, k_ext, v_ext, k_ext_t, k0_t, dk_ext, dv_ext, p_a, ds_a, p_b, ds_b, parts, gparts,
    *, rows, reach, tail,
):
    @pl.when(pl.program_id(0) == 0)
    def _():
        fill_bias(pos_ref, count_ref, prefix_ref, lens_ref, bias_a, bias_b, rows, reach, tail)

    k_ext[:tail] = kx_ref[:tail]
    k_ext[tail:] = k_ref[...]
    v_ext[:tail] = vx_ref[:tail]
    v_ext[tail:] = v_ref[...]
    k_ext_t[:, :tail] = transposed(kx_ref[:tail])
    k_ext_t[:, tail:] = transposed(k_ref[...])
    k0_t[...] = transposed(kx_ref[tail:])
    dk_ext[...] = jnp.zeros_like(dk_ext)
    dv_ext[...] = jnp.zeros_like(dv_ext)
    scale = HD**-0.5
    for b in range(rows // BQ):
        at = slice(BQ * b, BQ * b + BQ)
        both = slice(2 * BQ * b, 2 * BQ * b + 2 * BQ)
        band = slice(BQ * b, BQ * b + BQ + tail)
        part = both_heads(q_ref[at, :] * jnp.asarray(scale, bf16))
        gpart = both_heads(g_ref[at, :])
        parts[both, :] = part
        gparts[both, :] = gpart
        inner = turned_ref[0, b] * g_ref[at, :].astype(f32).T
        inner = jnp.concatenate(
            [
                jnp.sum(inner[:HD], axis=0, keepdims=True),
                jnp.sum(inner[HD:], axis=0, keepdims=True),
            ],
            axis=1,
        )
        lse = lse_ref[0, b]
        for first, keys, biased in key_chunks(reach, tail, b):
            there = slice(tail + keys.start, tail + keys.stop)
            k = kx_ref[there] if first else k_ext[keys, :]
            v = vx_ref[there] if first else v_ext[keys, :]
            bias = bias_a[b, biased] if first else bias_b[b, biased]
            p = jnp.exp(dot(k, part, NT) + twice(bias) - lse)
            ds = (p * (dot(v, gpart, NT) - inner)).astype(bf16)
            if first:
                p_a[keys, both] = p.astype(bf16)
                ds_a[keys, both] = ds
            else:
                p_b[biased, both] = p.astype(bf16)
                ds_b[biased, both] = ds
        dv_ext[band, :] += dot(p_b[:, both], gpart, NN)
        dk_ext[band, :] += dot(ds_b[:, both], part, NN)
        o = dot(k0_t[...], ds_a[:, both], NN) + dot(k_ext_t[:, band], ds_b[:, both], NN)
        o = jnp.concatenate([o[:HD, :BQ], o[HD:, BQ:]], axis=0) * scale
        dq_ref[at, :] = o.T.astype(bf16)
    dkx_ref[tail:] = dot(ds_a[...], parts[...], NN).astype(bf16)
    dvx_ref[tail:] = dot(p_a[...], gparts[...], NN).astype(bf16)
    dkx_ref[:tail] = dk_ext[:tail].astype(bf16)
    dvx_ref[:tail] = dv_ext[:tail].astype(bf16)
    dk_ref[...] = dk_ext[tail:].astype(bf16)
    dv_ref[...] = dv_ext[tail:].astype(bf16)


def column_block(rows, offset=0):
    return pl.BlockSpec((rows, 128), lambda i, *_: (0, offset + i))


def attend(scalars, qkv, kvx, rows, reach, tail):
    width = qkv.shape[1] // 3
    steps = width // 128
    blocks = rows // BQ
    extra = reach + tail
    return pl.pallas_call(
        functools.partial(attend_kernel, rows=rows, reach=reach, tail=tail),
        grid_spec=pltpu.PrefetchScalarGridSpec(
            num_scalar_prefetch=4,
            grid=(steps,),
            in_specs=[
                column_block(rows),
                column_block(rows, steps),
                column_block(rows, 2 * steps),
                column_block(extra),
                column_block(extra, steps),
            ],
            out_specs=[
                column_block(rows),
                pl.BlockSpec((1, blocks, 128, BQ), lambda i, *_: (i, 0, 0, 0)),
                pl.BlockSpec((1, blocks, 1, 2 * BQ), lambda i, *_: (i, 0, 0, 0)),
            ],
            scratch_shapes=[
                pltpu.VMEM((blocks, reach, BQ), f32),
                pltpu.VMEM((blocks, tail + BQ, BQ), f32),
                pltpu.VMEM((tail + rows, 128), bf16),
                pltpu.VMEM((128, tail + rows), bf16),
                pltpu.VMEM((128, reach), bf16),
                pltpu.VMEM((2, reach + tail + BQ, 2 * BQ), f32),
            ],
        ),
        out_shape=[
            jax.ShapeDtypeStruct((rows, width), bf16),
            jax.ShapeDtypeStruct((steps, blocks, 128, BQ), f32),
            jax.ShapeDtypeStruct((steps, blocks, 1, 2 * BQ), f32),
        ],
        name="attend",
    )(*scalars, qkv, qkv, qkv, kvx, kvx)


def attend_back(scalars, qkv, kvx, grad, turned, lse, rows, reach, tail):
    width = qkv.shape[1] // 3
    steps = width // 128
    blocks = rows // BQ
    extra = reach + tail
    return pl.pallas_call(
        functools.partial(attend_back_kernel, rows=rows, reach=reach, tail=tail),
        grid_spec=pltpu.PrefetchScalarGridSpec(
            num_scalar_prefetch=4,
            grid=(steps,),
            in_specs=[
                column_block(rows),
                column_block(rows, steps),
                column_block(rows, 2 * steps),
                column_block(extra),
                column_block(extra, steps),
                column_block(rows),
                pl.BlockSpec((1, blocks, 128, BQ), lambda i, *_: (i, 0, 0, 0)),
                pl.BlockSpec((1, blocks, 1, 2 * BQ), lambda i, *_: (i, 0, 0, 0)),
            ],
            out_specs=[
                column_block(rows),
                column_block(rows),
                column_block(rows),
                column_block(extra),
                column_block(extra),
            ],
            scratch_shapes=[
                pltpu.VMEM((blocks, reach, BQ), f32),
                pltpu.VMEM((blocks, tail + BQ, BQ), f32),
                pltpu.VMEM((tail + rows, 128), bf16),
                pltpu.VMEM((tail + rows, 128), bf16),
                pltpu.VMEM((128, tail + rows), bf16),
                pltpu.VMEM((128, reach), bf16),
                pltpu.VMEM((tail + rows, 128), f32),
                pltpu.VMEM((tail + rows, 128), f32),
                pltpu.VMEM((reach, 2 * rows), bf16),
                pltpu.VMEM((reach, 2 * rows), bf16),
                pltpu.VMEM((tail + BQ, 2 * rows), bf16),
                pltpu.VMEM((tail + BQ, 2 * rows), bf16),
                pltpu.VMEM((2 * rows, 128), bf16),
                pltpu.VMEM((2 * rows, 128), bf16),
            ],
        ),
        out_shape=[
            jax.ShapeDtypeStruct((rows, width), bf16),
            jax.ShapeDtypeStruct((rows, width), bf16),
            jax.ShapeDtypeStruct((rows, width), bf16),
            jax.ShapeDtypeStruct((extra, width), bf16),
            jax.ShapeDtypeStruct((extra, width), bf16),
        ],
        name="attend_back",
    )(*scalars, qkv, qkv, qkv, kvx, kvx, grad, turned, lse)


def mask_of(side, me):
    return me[1] + side * (me[2] - me[1])


def slab_at(place, me):
    side = (place >> 2) ^ me[0]
    return (side << 2) | ((place & 3) ^ mask_of(side, me))


def place_of(slab, me):
    side = slab >> 2
    return ((side ^ me[0]) << 2) | ((slab & 3) ^ mask_of(side, me))


def slab_rows(result, me_ref, out_ref):
    for c in range(PIECES):
        out_ref[0, c ^ (me_ref[3]), :ROWS, :] = result[ROWS * c : ROWS * c + ROWS].astype(bf16)


def outer_kernel(me_ref, a_ref, b_ref, out_ref):
    slab_rows(dot(a_ref[...], b_ref[...], TN), me_ref, out_ref)


def outer_half(me, a, b, half):
    rows, many = a.shape
    wide = many // SLABS
    return pl.pallas_call(
        outer_kernel,
        grid_spec=pltpu.PrefetchScalarGridSpec(
            num_scalar_prefetch=1,
            grid=(4,),
            in_specs=[
                pl.BlockSpec((rows, wide), lambda r, me: (0, slab_at(r + 4 * half, me))),
                pl.BlockSpec(b.shape, lambda r, me: (0, 0)),
            ],
            out_specs=pl.BlockSpec((1, PIECES, ROWS, b.shape[1]), lambda r, me: (r, 0, 0, 0)),
        ),
        out_shape=jax.ShapeDtypeStruct((4, PIECES, ROWS, b.shape[1]), bf16),
        name="outer",
    )(me, a, b)


def mixed_kernel(
    me_ref, dqkv_ref, n_ref, dkvx_ref, nx_ref, att_ref, gb_ref, small_ref, out_ref, *, half
):
    o = slab_at(pl.program_id(0) + 4 * half, me_ref)

    @pl.when(o < 2)
    def _():
        slab_rows(dot(dqkv_ref[...], n_ref[...], TN), me_ref, out_ref)

    @pl.when((o >= 2) & (o < 6))
    def _():
        slab_rows(
            dot(dqkv_ref[...], n_ref[...], TN) + dot(dkvx_ref[...], nx_ref[...], TN),
            me_ref,
            out_ref,
        )

    @pl.when(o >= 6)
    def _():
        slab_rows(dot(att_ref[...], gb_ref[...], TN), me_ref, out_ref)

    for c in range(PIECES):
        value = small_ref[EXTRA * c : EXTRA * c + EXTRA] if c < 2 else jnp.zeros_like(small_ref[:EXTRA])
        out_ref[0, c ^ (me_ref[3]), ROWS:, :] = jnp.where(o == 0, value, 0.0).astype(bf16)


def mixed_half(me, dqkv, normed, dkvx, normed_x, attended, grad_branch, small, half):
    rows, width = normed.shape
    wide = width // 2

    def slab(r, me):
        return slab_at(r + 4 * half, me)

    whole = lambda x: pl.BlockSpec(x.shape, lambda r, me: (0, 0))
    return pl.pallas_call(
        functools.partial(mixed_kernel, half=half),
        grid_spec=pltpu.PrefetchScalarGridSpec(
            num_scalar_prefetch=1,
            grid=(4,),
            in_specs=[
                pl.BlockSpec((rows, wide), lambda r, me: (0, jnp.minimum(slab(r, me), 5))),
                whole(normed),
                pl.BlockSpec(
                    (dkvx.shape[0], wide), lambda r, me: (0, jnp.clip(slab(r, me) - 2, 0, 3))
                ),
                whole(normed_x),
                pl.BlockSpec((rows, wide), lambda r, me: (0, jnp.maximum(slab(r, me) - 6, 0))),
                whole(grad_branch),
                whole(small),
            ],
            out_specs=pl.BlockSpec(
                (1, PIECES, ROWS + EXTRA, width), lambda r, me: (r, 0, 0, 0)
            ),
        ),
        out_shape=jax.ShapeDtypeStruct((4, PIECES, ROWS + EXTRA, width), bf16),
        name="outer_mixed",
    )(me, dqkv, normed, dkvx, normed_x, attended, grad_branch, small)


def slab_of(me_ref, ref):
    pieces = [ref[0, c ^ me_ref[3], :ROWS, :].astype(f32) for c in range(PIECES)]
    return jnp.concatenate(pieces, axis=0)


def spread_kernel(me_ref, f_ref, g_ref, out_ref, *, turned):
    o = pl.program_id(0)
    for ref, mine in ((f_ref, (o >> 2) == me_ref[0]), (g_ref, (o >> 2) != me_ref[0])):

        @pl.when(mine)
        def _():
            slab = slab_of(me_ref, ref)
            out_ref[...] = slab.T if turned else slab


def half_specs(rows, width):
    def block(o, me, other):
        side = me[0] ^ other
        rest = jnp.where(side == 0, jnp.minimum(o, 3), jnp.maximum(o, 4))
        return (place_of(rest, me) & 3, 0, 0, 0)

    return [
        pl.BlockSpec((1, PIECES, rows, width), lambda o, me: block(o, me, 0)),
        pl.BlockSpec((1, PIECES, rows, width), lambda o, me: block(o, me, 1)),
    ]


def spread(me, near, far, turned):
    width = near.shape[-1]
    wide = PIECES * ROWS
    many = SLABS * wide
    return pl.pallas_call(
        functools.partial(spread_kernel, turned=turned),
        grid_spec=pltpu.PrefetchScalarGridSpec(
            num_scalar_prefetch=1,
            grid=(SLABS,),
            in_specs=half_specs(ROWS, width),
            out_specs=pl.BlockSpec((width, wide), lambda o, me: (0, o))
            if turned
            else pl.BlockSpec((wide, width), lambda o, me: (o, 0)),
        ),
        out_shape=jax.ShapeDtypeStruct((width, many) if turned else (many, width), f32),
        name="spread",
    )(me, near, far)


def mixed_spread_kernel(me_ref, f_ref, g_ref, qkv_ref, out_ref, small_ref):
    o = pl.program_id(0)
    for ref, mine in ((f_ref, (o >> 2) == me_ref[0]), (g_ref, (o >> 2) != me_ref[0])):

        @pl.when(mine & (o < 6))
        def _():
            qkv_ref[...] = slab_of(me_ref, ref).T

        @pl.when(mine & (o >= 6))
        def _():
            out_ref[...] = slab_of(me_ref, ref)

        @pl.when(mine & (o == 0))
        def _():
            for c in range(2):
                small_ref[EXTRA * c : EXTRA * c + EXTRA, :] = ref[0, c ^ me_ref[3], ROWS:, :].astype(f32)


def mixed_spread(me, near, far):
    width = near.shape[-1]
    wide = PIECES * ROWS
    return pl.pallas_call(
        mixed_spread_kernel,
        grid_spec=pltpu.PrefetchScalarGridSpec(
            num_scalar_prefetch=1,
            grid=(SLABS,),
            in_specs=half_specs(ROWS + EXTRA, width),
            out_specs=[
                pl.BlockSpec((width, wide), lambda o, me: (0, jnp.minimum(o, 5))),
                pl.BlockSpec((wide, width), lambda o, me: (jnp.maximum(o - 6, 0), 0)),
                pl.BlockSpec((2 * EXTRA, width), lambda o, me: (0, 0)),
            ],
        ),
        out_shape=[
            jax.ShapeDtypeStruct((width, 3 * width), f32),
            jax.ShapeDtypeStruct((width, width), f32),
            jax.ShapeDtypeStruct((2 * EXTRA, width), f32),
        ],
        name="mixed_spread",
    )(me, near, far)


def grp_pairs(step):
    return [(g, step(g)) for g in range(8)]


ROUTES = (
    ("grp", grp_pairs(lambda g: g ^ 1)),
    ("grp", grp_pairs(lambda g: g ^ (2 if g % 2 == 0 else 4))),
    ("grp", grp_pairs(lambda g: g ^ (4 if g % 2 == 0 else 2))),
    ("pos", [(p, p ^ 1) for p in range(4)]),
    ("pos", [(p, p ^ 2) for p in range(4)]),
)


def hop(value, step):
    axis, pairs = ROUTES[step]
    return lax.ppermute(value, axis, pairs)


def added(a, b):
    return (a.astype(f32) + b.astype(f32)).astype(bf16)


def tied(*values):
    return lax.optimization_barrier(values)


class Sum:
    def __init__(self, far, cube):
        self.shape = far.shape
        self.cube = cube
        self.stage = 0
        self.keep = None
        self.send = far.reshape((16,) + far.shape[2:])
        self.launch()

    def launch(self):
        if self.cube and self.stage < 10:
            self.got = hop(self.send, self.stage if self.stage < 5 else 9 - self.stage)

    def give(self, near):
        self.keep = near.reshape(self.send.shape)

    def settle(self):
        got = self.got
        half = self.keep.shape[0] // 2
        if self.stage < 4:
            self.send = added(self.keep[half:], got[half:])
            self.keep = added(self.keep[:half], got[:half])
        elif self.stage == 4:
            self.keep = self.send = added(self.keep, got)
        elif self.stage < 9:
            self.keep = self.send = jnp.concatenate([self.keep, got], axis=0)
        else:
            self.send = got
        self.stage += 1

    def halves(self):
        if not self.cube:
            near, far = lax.psum((self.keep, self.send), ("grp", "pos"))
            return near.reshape(self.shape), far.reshape(self.shape)
        while self.stage < 10:
            advance((), self)
        return self.keep.reshape(self.shape), self.send.reshape(self.shape)


def advance(values, *sums):
    sums = [one for one in sums if one.cube and one.stage < 10]
    for one in sums:
        one.settle()
    states = [(one.keep, one.send) for one in sums]
    values, states = tied(values, states)
    for one, (one.keep, one.send) in zip(sums, states):
        one.launch()
    return values


def return_first(partial, blocks, rows, cube):
    place = lax.axis_index("pos")
    if cube and blocks == 1:
        low = partial.astype(bf16)
        here = partial.astype(f32) + lax.ppermute(low, "pos", [(1, 0), (3, 2)]).astype(f32)
        got = lax.ppermute(here.astype(bf16), "pos", [(2, 0)])
        mine = here + got.astype(f32)
    else:
        total = lax.psum(partial.astype(bf16), "pos")
        at = jnp.minimum(place, blocks - 1) * rows
        mine = lax.dynamic_slice_in_dim(total, at, rows, axis=0).astype(f32)
    return jnp.where(place < blocks, mine, 0.0)


def body(
    hidden_in,
    ln1_gain,
    ln1_shift,
    w_qkv,
    b_query,
    b_value,
    w_out,
    b_out,
    ln2_gain,
    ln2_shift,
    w_up,
    b_up,
    w_down,
    b_down,
    cotangent,
    sol_count,
    prefix_len,
    sol_len,
):
    rows, width = hidden_in.shape
    n_pos = lax.axis_size("pos")
    n_grp = lax.axis_size("grp")
    cube = n_grp == 8 and n_pos == 4
    set_length = rows * n_pos
    blocks = -(-(set_length // 4) // rows)
    reach = blocks * rows
    tail = -(-(3 * set_length // 64) // BQ) * BQ

    place = lax.axis_index("pos")
    if cube:
        g = lax.axis_index("grp")
        core, x, y = g & 1, (g >> 1) & 1, (g >> 2) & 1
        me = jnp.stack([core, 2 * x + y, 2 * y + x, 2 * (place & 1) + (place >> 1)])
    else:
        me = jnp.zeros((4,), jnp.int32)
    me = me.astype(jnp.int32)
    scalars = (place.astype(jnp.int32).reshape(1), sol_count, prefix_len, sol_len)

    gain1, shift1 = ln1_gain.astype(f32), ln1_shift.astype(f32)
    gain2, shift2 = ln2_gain.astype(f32), ln2_shift.astype(f32)

    tail_in = lax.ppermute(
        hidden_in[rows - tail :], "pos", [(p, p + 1) for p in range(n_pos - 1)]
    )
    two_step = cube and blocks == 1
    if two_step:
        got = lax.ppermute(hidden_in, "pos", [(0, 2)])
    else:
        got = lax.all_gather(hidden_in, "pos", axis=0, tiled=True)[: blocks * rows]

    inputs = hidden_in.astype(f32)
    xhat1, inv1 = norm_stats(inputs)
    normed1 = (xhat1 * gain1 + shift1).astype(bf16)
    bias = jnp.concatenate([b_query.astype(f32), jnp.zeros((width,), f32), b_value.astype(f32)])
    qkv = (dot(normed1, w_qkv, NN) + bias).astype(bf16)
    qkv, got, cotangent = tied(qkv, got, cotangent)
    if two_step:
        here = jnp.where(place == 2, got, hidden_in)
        got = lax.ppermute(here, "pos", [(0, 1), (2, 3)])
    grad_activ = dot(cotangent, w_down, NT)
    grad_activ, got, tail_in = tied(grad_activ, got, tail_in)
    first_in = jnp.where(place % 2 == 1, got, here) if two_step else got

    inputs_x = jnp.concatenate([tail_in, first_in], axis=0).astype(f32)
    xhat1_x, _ = norm_stats(inputs_x)
    normed1_x = (xhat1_x * gain1 + shift1).astype(bf16)
    kvx = (dot(normed1_x, w_qkv[:, width:], NN) + bias[width:]).astype(bf16)

    attended, turned, lse = attend(scalars, qkv, kvx, rows, reach, tail)

    middle = inputs + dot(attended, w_out, NN) + b_out.astype(f32)
    xhat2, inv2 = norm_stats(middle)
    normed2 = (xhat2 * gain2 + shift2).astype(bf16)
    pre_act = dot(normed2, w_up, NN) + b_up.astype(f32)
    activ, gelu_pull = jax.vjp(gelu_tanh, pre_act)
    activ = activ.astype(bf16)

    down_far = outer_half(me, activ, cotangent, 1)
    down_far, activ, cotangent, grad_activ = tied(down_far, activ, cotangent, grad_activ)
    down = Sum(down_far, cube)
    down.give(outer_half(me, activ, cotangent, 0))
    grad_activ, activ = advance((grad_activ, activ), down)

    grad_pre = gelu_pull(grad_activ)[0].astype(bf16)
    up_far = outer_half(me, grad_pre, normed2, 1)
    up_far, grad_pre, normed2 = tied(up_far, grad_pre, normed2)
    up = Sum(up_far, cube)
    grad_pre, normed2 = advance((grad_pre, normed2), down)
    up.give(outer_half(me, grad_pre, normed2, 0))
    (grad_pre,) = advance((grad_pre,), up)

    grad_normed2 = dot(grad_pre, w_up, NT)
    grad_middle = cotangent.astype(f32) + norm_back(grad_normed2, gain2, xhat2, inv2)
    grad_branch = grad_middle.astype(bf16)
    grad_attended = dot(grad_branch, w_out, NT).astype(bf16)
    (grad_attended,) = advance((grad_attended,), down)
    grads = attend_back(scalars, qkv, kvx, grad_attended, turned, lse, rows, reach, tail)
    dq, dk, dv, dkx, dvx = advance(grads, down, up)
    dqkv = jnp.concatenate([dq, dk, dv], axis=1)
    dkvx = jnp.concatenate([dkx, dvx], axis=1)
    grad_normed1 = dot(dqkv, w_qkv, NT)
    grad_normed1_x = dot(dkvx, w_qkv[:, width:], NT)
    grad_normed1, grad_normed1_x = advance((grad_normed1, grad_normed1_x), down, up)

    back_tail = lax.ppermute(
        grad_normed1_x[:tail].astype(bf16), "pos", [(p + 1, p) for p in range(n_pos - 1)]
    )

    small = jnp.concatenate(
        [
            column_sum(cotangent),
            column_sum(grad_pre),
            column_sum(grad_normed2 * xhat2),
            column_sum(grad_normed2),
            column_sum(grad_branch),
            column_sum(dq),
            column_sum(dv) + column_sum(dvx),
            column_sum(grad_normed1 * xhat1) + column_sum(grad_normed1_x * xhat1_x),
            column_sum(grad_normed1) + column_sum(grad_normed1_x),
            jnp.zeros((4 * width,), f32),
        ]
    ).reshape(2 * EXTRA, width)
    mixed_args = (me, dqkv, normed1, dkvx, normed1_x, attended, grad_branch, small)
    mixed_far = mixed_half(*mixed_args, 1)
    (mixed_far,) = advance((mixed_far,), down, up)
    mixed = Sum(mixed_far, cube)
    mixed.give(mixed_half(*mixed_args, 0))
    advance((), mixed, up)
    advance((), mixed)
    advance((), mixed, down, up)

    back_first = return_first(grad_normed1_x[tail:], blocks, rows, cube)
    grad_normed1 = (
        grad_normed1
        + back_first
        + jnp.concatenate([jnp.zeros((rows - tail, width), f32), back_tail.astype(f32)], axis=0)
    )
    input_grad = (grad_middle + norm_back(grad_normed1, gain1, xhat1, inv1)).astype(bf16)

    layer_out = (middle + dot(activ, w_down, NN) + b_down.astype(f32)).astype(bf16)

    grad_w_down = spread(me, *down.halves(), False)
    grad_w_up = spread(me, *up.halves(), True)
    grad_w_qkv, grad_w_out, vectors = mixed_spread(me, *mixed.halves())
    return (
        layer_out,
        input_grad,
        vectors[10],
        vectors[11],
        grad_w_qkv,
        vectors[8],
        vectors[9],
        grad_w_out,
        vectors[7],
        vectors[5],
        vectors[6],
        grad_w_up,
        vectors[1:5].reshape(-1),
        grad_w_down,
        vectors[0],
    )


def solution(mesh):
    rows = P(("grp", "pos"), None)
    placed = (rows,) + (P(),) * 13 + (rows, P("grp"), P("grp"), P("grp", None))
    return jax.shard_map(
        body,
        mesh=mesh,
        in_specs=placed,
        out_specs=(rows, rows) + (P(),) * 13,
        check_vma=False,
    )
```
